32 devices in a mesh: lat: 4 (over y, x), lon: 8 (over z, core).
Axes of the slice: x: 2, y: 2, z: 4, core: 2. Of those that a mesh axis runs over, the one named last changes fastest.
Arguments:
- signal: bfloat16 [96, 144, 512], P('lat', 'lon'), may hold values from -6 to 6
- band_rows: int32 [4], replicated, may hold values from 12 to 24, as said below
- support_rows: int32 [72, 16], replicated, may hold values from 0 to 71, as said below
- support_lons: int32 [72, 16], replicated, may hold values from 0 to 143, as said below
- basis_values: bfloat16 [72, 16, 9], replicated, may hold values from -1.5 to 1.5
- mixing: bfloat16 [9, 512, 512], P(None, 'lon'), may hold values from -0.09375 to 0.09375
Outputs:
- convolved: bfloat16 [96, 144, 512], P('lat', 'lon')
The draws below stay inside these ranges and needn't reach their ends.
Inputs may be any that keep to these rules, and one draw needn't show every extreme that they name: `band_rows`: the counts sum to 72; the largest is 24. `support_rows`: every entry of grid row i lies within 2 rows of i. `support_lons`: for rows i with 2 <= i < 70, each offset is at most 2 or at least 142; rows nearer a pole may take any offset.
All inputs are finite; a program needn't handle non-finite values.
Results may differ from the reference program's by a relative error of at most 0.0049.
Values may be sent and summed in bfloat16 or wider, within the bound.
A program may use at most 64 MiB of HBM per device.

```python
import jax
import jax.numpy as jnp
from jax import lax

CHANNELS = 512
OUT_CHANNELS = 512
BASIS = 9
SUPPORT = 16
LAT_REACH = 2
LON_REACH = 2
POLAR_ROWS = 2
ROWS_DEV = 24
LON_DEV = 18
GRID_ROWS = 72
GRID_LONS = 144
SLOTS = 96
N_LAT = 4
N_LON = 8


def support_tables(key):
    base_key = jax.random.fold_in(key, 11)
    sub_keys = jax.random.split(base_key, 5)
    cycle_len = LON_DEV * N_LON
    grid_ids = jnp.arange(GRID_ROWS, dtype=jnp.int32)[:, None]
    row_steps = jax.random.randint(sub_keys[0], (GRID_ROWS, SUPPORT), -LAT_REACH, LAT_REACH + 1)
    col_steps = jax.random.randint(sub_keys[1], (GRID_ROWS, SUPPORT), -LON_REACH, LON_REACH + 1)
    first_pick = jax.random.randint(sub_keys[2], (GRID_ROWS, 1), 0, SUPPORT)
    second_pick = (first_pick + 1 + jax.random.randint(sub_keys[3], (GRID_ROWS, 1), 0, SUPPORT - 1)) % SUPPORT
    entry_ids = jnp.arange(SUPPORT, dtype=jnp.int32)[None, :]
    row_steps = jnp.where(entry_ids == first_pick, LAT_REACH, jnp.where(entry_ids == second_pick, -LAT_REACH, row_steps))
    col_steps = jnp.where(entry_ids == first_pick, LON_REACH, jnp.where(entry_ids == second_pick, -LON_REACH, col_steps))
    near_pole = (grid_ids < POLAR_ROWS) | (grid_ids >= GRID_ROWS - POLAR_ROWS)
    wide_steps = jax.random.randint(sub_keys[4], (GRID_ROWS, SUPPORT), 0, cycle_len)
    source_lons = jnp.where(near_pole, wide_steps, col_steps % cycle_len)
    source_rows = jnp.clip(grid_ids + row_steps, 0, GRID_ROWS - 1)
    return (source_rows.astype(jnp.int32), source_lons.astype(jnp.int32))


def draw_support_rows(key, part):
    return support_tables(key)[0]


def draw_support_lons(key, part):
    return support_tables(key)[1]


def draw_band_rows(key, part):
    sub_keys = jax.random.split(jax.random.fold_in(key, 7), 2)
    lower_count = ROWS_DEV // 2
    spare_rows = ROWS_DEV - lower_count
    fullest = jax.random.randint(sub_keys[0], (), 0, N_LAT)
    unit_total = N_LAT * spare_rows
    unit_band = jnp.arange(unit_total, dtype=jnp.int32) // spare_rows
    scores = jax.random.permutation(sub_keys[1], unit_total).astype(jnp.int32)
    scores = jnp.where(unit_band == fullest, unit_total + jnp.arange(unit_total, dtype=jnp.int32), scores)
    unit_ranks = jnp.argsort(jnp.argsort(scores))
    remaining = GRID_ROWS - N_LAT * lower_count - spare_rows
    chosen = (unit_ranks < remaining).astype(jnp.int32)
    band_ids = jnp.arange(N_LAT, dtype=jnp.int32)
    extra_rows = jnp.sum(jnp.where(unit_band[None, :] == band_ids[:, None], chosen[None, :], 0), axis=1)
    return (lower_count + extra_rows + jnp.where(band_ids == fullest, spare_rows, 0)).astype(jnp.int32)


def levels(stream_key, dims, shards, least, high):
    gain = 1.0
    for axis_at, parts in shards:
        heights = jax.random.uniform(jax.random.fold_in(jax.random.fold_in(stream_key, 6), axis_at), (parts,), jnp.float32, least / len(shards), high / len(shards))
        gain = gain * jnp.repeat(jnp.exp(heights), dims[axis_at] // parts).reshape((-1,) + (1,) * (len(dims) - 1 - axis_at))
    return gain


def scatter_about(key, dims, spread, most, shards=(), kind=jnp.bfloat16):
    values = spread * jax.random.normal(key, dims, jnp.float32)
    if shards:
        values = values * levels(key, dims, shards, -0.22, 0.18)
    return jnp.clip(values, -most, most).astype(kind)


def setup_inputs(seed: int = 0) -> dict:
    seeds = jax.random.split(jax.random.key(seed), 7)
    return {
        "signal": scatter_about(seeds[0], (SLOTS, GRID_LONS, CHANNELS), 1.0, 6.0, ((0, 4), (1, 8))),
        "band_rows": draw_band_rows(jax.random.fold_in(seeds[6], 71), 0),
        "support_rows": draw_support_rows(jax.random.fold_in(seeds[6], 71), 0),
        "support_lons": draw_support_lons(jax.random.fold_in(seeds[6], 71), 0),
        "basis_values": scatter_about(seeds[4], (GRID_ROWS, SUPPORT, BASIS), SUPPORT ** -0.5, 1.5),
        "mixing": scatter_about(seeds[5], (BASIS, CHANNELS, OUT_CHANNELS), (BASIS * CHANNELS) ** -0.5, 0.09375, ((1, 8),)),
    }


def reference(signal, band_rows, support_rows, support_lons, basis_values, mixing):
    starts = jnp.cumsum(band_rows) - band_rows
    grid_ids = jnp.arange(GRID_ROWS, dtype=jnp.int32)
    owner_band = jnp.sum((starts[None, :] <= grid_ids[:, None]).astype(jnp.int32), axis=1) - 1
    slot_of_row = (owner_band * ROWS_DEV + grid_ids - starts[owner_band]).astype(jnp.int32)
    columns = jnp.arange(GRID_LONS, dtype=jnp.int32)

    def one_slot(slot_id):
        slot_band = slot_id // ROWS_DEV
        position = slot_id % ROWS_DEV
        grid_id = jnp.clip(starts[slot_band] + position, 0, GRID_ROWS - 1).astype(jnp.int32)
        sources = slot_of_row[support_rows[grid_id]]
        shifted = (columns[None, :] + support_lons[grid_id][:, None]) % GRID_LONS
        pieces = signal[sources[:, None], shifted].astype(jnp.float32)
        basis_terms = jnp.einsum("sk,snc->knc", basis_values[grid_id].astype(jnp.float32), pieces)
        basis_terms = lax.optimization_barrier(basis_terms.astype(jnp.bfloat16))
        mixed_row = jnp.einsum("knc,kco->no", basis_terms.astype(jnp.float32), mixing.astype(jnp.float32))
        keep_row = position < band_rows[slot_band]
        return jnp.where(keep_row, mixed_row, jnp.zeros_like(mixed_row)).astype(jnp.bfloat16)

    return lax.map(one_slot, jnp.arange(N_LAT * ROWS_DEV, dtype=jnp.int32))
```

```python
import functools

import jax
import jax.numpy as jnp
from jax import lax
from jax.experimental import pallas as pl
from jax.experimental.pallas import tpu as pltpu
from jax.sharding import PartitionSpec as P

LAT_REACH = 2
LON_REACH = 2
POLAR_ROWS = 2
SPAN = POLAR_ROWS + LAT_REACH
GROUP = 4
PAD = 24
WIDE = 32
PIECES = 4
CHUNKS = 3
POLAR_PAD = 80
MESH = pl.DeviceIdType.MESH
BF16 = jnp.bfloat16
F32 = jnp.float32


def rdma(src, dst, send_sem, recv_sem, lat, lon):
    return pltpu.make_async_remote_copy(
        src_ref=src, dst_ref=dst, send_sem=send_sem, recv_sem=recv_sem,
        device_id=(lat, lon), device_id_type=MESH,
    )


def kernel(
    n_lat, n_lon, grid_rows,
    signal, band_rows, sup_rows, sup_lons, basis, mixing, out,
    full_w, a_band, z_all, acc, ext, rim_send, rim_up, rim_down,
    edge_send, edge_recv, pol_send, pol, a_pol, z_pol,
    s1_send, s1_recv, s2_send, s2_recv, s3_send, s3_recv,
    rim_ss, rim_rs, edge_ss, edge_rs, p1_ss, p1_rs, p2_ss, p2_rs, own_sem,
):
    rows_dev, lon_dev, channels = signal.shape
    n_basis, c_dev, _ = mixing.shape
    support = sup_rows.shape[1]
    cycle = lon_dev * n_lon
    n_group = rows_dev // GROUP
    lat = lax.axis_index("lat")
    lon = lax.axis_index("lon")
    is_top = lat == 0
    is_bottom = lat == n_lat - 1
    is_polar = is_top | is_bottom
    sub = lat % PIECES
    lat_base = lat - sub
    peers = n_lon // 2
    partner = lon + 1 - 2 * (lon % 2)
    right = (lon + 1) % n_lon
    left = (lon + n_lon - 1) % n_lon
    ks = n_basis // CHUNKS

    live = band_rows[lat]
    first_row = 0
    for b in range(n_lat):
        first_row = first_row + jnp.where(b < lat, band_rows[b], 0)

    barrier = pltpu.get_barrier_semaphore()
    for d in range(1, peers):
        pl.semaphore_signal(barrier, inc=1, device_id=(lat, (lon + 2 * d) % n_lon), device_id_type=MESH)
    for e in range(1, PIECES):
        pl.semaphore_signal(barrier, inc=1, device_id=(lat_base + (sub + e) % PIECES, lon), device_id_type=MESH)
    pl.semaphore_signal(barrier, inc=1, device_id=(lat, right), device_id_type=MESH)
    pl.semaphore_signal(barrier, inc=1, device_id=(lat, left), device_id_type=MESH)

    @pl.when(lat > 0)
    def _():
        pl.semaphore_signal(barrier, inc=1, device_id=(lat - 1, lon), device_id_type=MESH)

    @pl.when(lat < n_lat - 1)
    def _():
        pl.semaphore_signal(barrier, inc=1, device_id=(lat + 1, lon), device_id_type=MESH)

    rim_send[...] = signal[pl.ds(jnp.clip(live - LAT_REACH, 0, rows_dev - LAT_REACH), LAT_REACH)]
    polar_start = jnp.where(is_bottom, jnp.clip(live - SPAN, 0, rows_dev - SPAN), 0)
    pol_rows = [signal[polar_start + r] for r in range(SPAN)]
    tail = jnp.zeros((POLAR_PAD - SPAN * lon_dev, channels), BF16)
    pol_send[...] = jnp.concatenate(pol_rows + [tail], axis=0)
    for r in range(rows_dev):
        edge_send[0, r] = signal[r, 0:LON_REACH]
        edge_send[1, r] = signal[r, lon_dev - LON_REACH : lon_dev]

    greeted = (peers - 1) + (PIECES - 1) + 2
    pl.semaphore_wait(barrier, greeted + jnp.where(lat > 0, 1, 0) + jnp.where(lat < n_lat - 1, 1, 0))

    def rows_of(source):
        return pl.ds(pl.multiple_of(source * c_dev, c_dev), c_dev)

    def lanes_of(piece):
        return pl.ds(pl.multiple_of(piece * 128, 128), 128)

    mine = rows_of(lon)
    q = lanes_of(sub)

    def stage1(d, j):
        kk = pl.ds(j * ks, ks)
        return rdma(
            mixing.at[kk, :, q], full_w.at[kk, mine, q], s1_send.at[d - 1, j], s1_recv.at[d - 1, j],
            lat, (lon + 2 * d) % n_lon,
        )

    def stage2(e, d, j):
        kk = pl.ds(j * ks, ks)
        region = full_w.at[kk, rows_of((lon + n_lon - 2 * d) % n_lon), q]
        return rdma(
            region, region, s2_send.at[e - 1, d - 1, j], s2_recv.at[e - 1, d - 1, j],
            lat_base + (sub + e) % PIECES, lon,
        )

    def stage3(d, j):
        kk = pl.ds(j * ks, ks)
        region = full_w.at[kk, rows_of((lon + n_lon - 2 * d) % n_lon), :]
        source = mixing.at[kk] if d == 0 else region
        return rdma(source, region, s3_send.at[d, j], s3_recv.at[d, j], lat, partner)

    up_copy = rdma(signal.at[pl.ds(0, LAT_REACH)], rim_down, rim_ss.at[0], rim_rs.at[0], lat - 1, lon)
    down_copy = rdma(rim_send, rim_up, rim_ss.at[1], rim_rs.at[1], lat + 1, lon)

    @pl.when(lat > 0)
    def _():
        up_copy.start()

    @pl.when(lat < n_lat - 1)
    def _():
        down_copy.start()

    for j in range(CHUNKS):
        for d in range(1, peers):
            stage1(d, j).start()
        stage3(0, j).start()
    own_copy = pltpu.make_async_copy(mixing, full_w.at[:, mine, :], own_sem)
    own_copy.start()

    def polar1(d):
        return rdma(pol_send, pol.at[lon, pl.ds(0, POLAR_PAD)], p1_ss.at[d - 1], p1_rs.at[d - 1], lat, (lon + 2 * d) % n_lon)

    def polar2(d):
        region = pol.at[(lon + n_lon - 2 * d) % n_lon, pl.ds(0, POLAR_PAD)]
        source = pol_send if d == 0 else region
        return rdma(source, region, p2_ss.at[d], p2_rs.at[d], lat, partner)

    @pl.when(is_top)
    def _():
        rim_up[...] = jnp.zeros_like(rim_up)

    @pl.when(is_bottom)
    def _():
        rim_down[...] = jnp.zeros_like(rim_down)

    @pl.when(is_polar)
    def _():
        for d in range(1, peers):
            polar1(d).start()
        polar2(0).start()
        pol[lon, pl.ds(0, POLAR_PAD)] = pol_send[...]
        for b in range(n_lon):
            pol[b, pl.ds(POLAR_PAD, 128 - POLAR_PAD)] = jnp.zeros((128 - POLAR_PAD, channels), BF16)

    col = lax.broadcasted_iota(jnp.int32, (PAD, 128), 1)
    pos = lax.broadcasted_iota(jnp.int32, (PAD, 128), 0)
    within = col % WIDE
    target = jnp.where(within < lon_dev, within, jnp.where(within < lon_dev + LON_REACH, within - lon_dev - LON_REACH, within - LON_REACH))
    code0 = jnp.where(within < lon_dev + 2 * LON_REACH, (col // WIDE) * 64 + target - pos + LON_REACH, -100000)
    half_rows = 128 // WIDE

    def accumulate(code, keys, grid_id):
        sums = [jnp.zeros((PAD, 128), F32) for _ in range(n_basis)]
        for s in range(support):
            hit = code == keys[s]
            for k in range(n_basis):
                sums[k] = sums[k] + jnp.where(hit, basis[grid_id, s * n_basis + k], 0.0)
        return sums

    def build_slot(i, carry):
        g = i // GROUP
        r = i % GROUP
        grid_id = jnp.minimum(first_row + i, grid_rows - 1)
        keys = []
        for s in range(support):
            off = sup_lons[grid_id, s]
            off = jnp.where(off > cycle // 2, off - cycle, off)
            window = sup_rows[grid_id, s] - first_row + LAT_REACH - g * GROUP
            keys.append(window * 64 + off + LON_REACH)
        for h in range(2):
            sums = accumulate(code0, [key - h * half_rows * 64 for key in keys], grid_id)
            for k in range(n_basis):
                a_band[g, k, pl.ds(pl.multiple_of(r * PAD, PAD), PAD), h * 128 : (h + 1) * 128] = sums[k]
        return carry

    def forward2(j):
        for d in range(1, peers):
            stage1(d, j).wait_recv()
            for e in range(1, PIECES):
                stage2(e, d, j).start()

    def forward3(j):
        for d in range(1, peers):
            for e in range(1, PIECES):
                stage2(e, d, j).wait_recv()
            stage3(d, j).start()

    lax.fori_loop(0, 4, build_slot, 0)

    @pl.when(lat > 0)
    def _():
        down_copy.wait_recv()

    @pl.when(lat < n_lat - 1)
    def _():
        up_copy.wait_recv()

    for r in range(LAT_REACH):
        edge_send[0, rows_dev + r] = rim_up[r, 0:LON_REACH]
        edge_send[1, rows_dev + r] = rim_up[r, lon_dev - LON_REACH : lon_dev]
        edge_send[0, rows_dev + LAT_REACH + r] = rim_down[r, 0:LON_REACH]
        edge_send[1, rows_dev + LAT_REACH + r] = rim_down[r, lon_dev - LON_REACH : lon_dev]
    lax.fori_loop(4, 6, build_slot, 0)
    to_left = rdma(edge_send.at[0], edge_recv.at[1], edge_ss.at[0], edge_rs.at[0], lat, left)
    to_right = rdma(edge_send.at[1], edge_recv.at[0], edge_ss.at[1], edge_rs.at[1], lat, right)
    to_left.start()
    to_right.start()
    forward2(0)
    lax.fori_loop(6, 14, build_slot, 0)
    forward2(1)
    lax.fori_loop(14, rows_dev, build_slot, 0)

    @pl.when(is_polar)
    def _():
        for d in range(1, peers):
            polar1(d).wait_recv()
            polar2(d).start()

    forward2(2)
    forward3(0)

    to_left.wait_recv()
    to_right.wait_recv()

    def source_row(slot, own, rim_u, rim_d):
        if slot < 0:
            return rim_u(slot + LAT_REACH)
        base = own(min(slot, rows_dev - 1))
        if slot < rows_dev // 2:
            return base
        value = jnp.where(live == slot, rim_d(0), base)
        return jnp.where(live + 1 == slot, rim_d(1), value)

    filler = jnp.zeros((WIDE - lon_dev - 2 * LON_REACH, channels), BF16)
    for e in range(rows_dev + 2 * LAT_REACH):
        centre = source_row(e - LAT_REACH, lambda r: signal[r], lambda r: rim_up[r], lambda r: rim_down[r])
        sides = [
            source_row(
                e - LAT_REACH,
                lambda r: edge_recv[side, r],
                lambda r: edge_recv[side, rows_dev + r],
                lambda r: edge_recv[side, rows_dev + LAT_REACH + r],
            )
            for side in range(2)
        ]
        ext[e] = jnp.concatenate([centre, sides[0], sides[1], filler], axis=0)

    out_base = jnp.where(is_bottom, grid_rows - POLAR_ROWS, 0)
    src_base = jnp.where(is_bottom, grid_rows - SPAN, 0)

    @pl.when(is_polar)
    def _():
        for d in range(peers):
            polar2(d).wait_recv()
        z_pol[...] = jnp.zeros_like(z_pol)
        prow = jnp.where(col >= lon_dev, 1, 0) + jnp.where(col >= 2 * lon_dev, 1, 0) + jnp.where(col >= 3 * lon_dev, 1, 0)
        pcol = col - prow * lon_dev

        def polar_block(b, carry):
            shift = pcol - pos + (b - lon) * lon_dev
            shift = jnp.where(shift < 0, shift + cycle, shift)
            code = jnp.where(col < SPAN * lon_dev, prow * cycle + shift, -100000)
            for r in range(POLAR_ROWS):
                grid_id = out_base + r
                keys = [(sup_rows[grid_id, s] - src_base) * cycle + sup_lons[grid_id, s] for s in range(support)]
                sums = accumulate(code, keys, grid_id)
                for k in range(n_basis):
                    a_pol[pl.ds((r * n_basis + k) * PAD, PAD), :] = sums[k]
            z_pol[...] += jnp.dot(a_pol[...].astype(BF16), pol[b], preferred_element_type=F32)
            return carry

        lax.fori_loop(0, n_lon, polar_block, 0)

    forward3(1)
    polar_slot = jnp.where(is_top, 0, jnp.where(is_bottom, live - POLAR_ROWS, -100))
    span_rows = GROUP * PAD
    group_slot = lax.broadcasted_iota(jnp.int32, (span_rows, channels), 0) // PAD

    def apply_group(g, carry):
        a_now = a_band[g].reshape(n_basis * span_rows, 256).astype(BF16)
        window = ext[pl.ds(g * GROUP, 2 * GROUP)].reshape(256, channels)
        terms = jnp.dot(a_now, window, preferred_element_type=F32)
        for k in range(n_basis):
            value = terms[k * span_rows : (k + 1) * span_rows]
            for r in range(POLAR_ROWS):
                chosen = z_pol[pl.ds((r * n_basis + k) * PAD, PAD), :]
                chosen = jnp.concatenate([chosen] * GROUP, axis=0)
                value = jnp.where(group_slot == polar_slot + r - g * GROUP, chosen, value)
            z_all[pl.ds(pl.multiple_of(g * span_rows, span_rows), span_rows), k * channels : (k + 1) * channels] = value.astype(BF16)
        return carry

    lax.fori_loop(0, n_group, apply_group, 0)
    forward3(2)

    own_copy.wait()
    half_m = rows_dev * PAD // 2
    acc[...] = jnp.zeros_like(acc)
    for j in range(CHUNKS):
        for d in range(peers):
            stage3(d, j).wait_recv()

        def mix(t, carry):
            k = j * ks + t // 2
            rows = pl.ds(pl.multiple_of((t % 2) * half_m, half_m), half_m)
            lhs = z_all[rows, pl.ds(pl.multiple_of(k * channels, channels), channels)]
            acc[rows, :] += jnp.dot(lhs, full_w[k], preferred_element_type=F32)
            return carry

        lax.fori_loop(0, 2 * ks, mix, 0)

    def put(i, carry):
        value = acc[pl.ds(pl.multiple_of(i * PAD, PAD), PAD), :]
        value = jnp.where(i < live, value, 0.0)
        out[i] = value[0:lon_dev].astype(BF16)
        return carry

    lax.fori_loop(0, rows_dev, put, 0)

    to_left.wait_send()
    to_right.wait_send()

    @pl.when(lat > 0)
    def _():
        up_copy.wait_send()

    @pl.when(lat < n_lat - 1)
    def _():
        down_copy.wait_send()

    @pl.when(is_polar)
    def _():
        for d in range(peers):
            if d:
                polar1(d).wait_send()
            polar2(d).wait_send()

    for j in range(CHUNKS):
        for d in range(peers):
            stage3(d, j).wait_send()
            if d:
                stage1(d, j).wait_send()
                for e in range(1, PIECES):
                    stage2(e, d, j).wait_send()


def solution(mesh):
    n_lat, n_lon = mesh.shape["lat"], mesh.shape["lon"]

    def per_device(signal, band_rows, support_rows, support_lons, basis_values, mixing):
        rows_dev, lon_dev, channels = signal.shape
        n_basis, c_dev, outs = mixing.shape
        grid_rows, support = support_rows.shape
        peers = n_lon // 2
        table = basis_values.astype(F32).reshape(grid_rows, support * n_basis)
        vmem = pl.BlockSpec(memory_space=pltpu.VMEM)
        smem = pl.BlockSpec(memory_space=pltpu.SMEM)
        dma = pltpu.SemaphoreType.DMA
        return pl.pallas_call(
            functools.partial(kernel, n_lat, n_lon, grid_rows),
            out_shape=jax.ShapeDtypeStruct((rows_dev, lon_dev, outs), BF16),
            in_specs=[vmem, smem, smem, smem, smem, vmem],
            out_specs=vmem,
            scratch_shapes=[
                pltpu.VMEM((n_basis, n_lon * c_dev, outs), BF16),
                pltpu.VMEM((rows_dev // GROUP, n_basis, GROUP * PAD, 256), F32),
                pltpu.VMEM((rows_dev * PAD, n_basis * channels), BF16),
                pltpu.VMEM((rows_dev * PAD, outs), F32),
                pltpu.VMEM((rows_dev + 2 * LAT_REACH, WIDE, channels), BF16),
                pltpu.VMEM((LAT_REACH, lon_dev, channels), BF16),
                pltpu.VMEM((LAT_REACH, lon_dev, channels), BF16),
                pltpu.VMEM((LAT_REACH, lon_dev, channels), BF16),
                pltpu.VMEM((2, rows_dev + 2 * LAT_REACH, LON_REACH, channels), BF16),
                pltpu.VMEM((2, rows_dev + 2 * LAT_REACH, LON_REACH, channels), BF16),
                pltpu.VMEM((POLAR_PAD, channels), BF16),
                pltpu.VMEM((n_lon, 128, channels), BF16),
                pltpu.VMEM((POLAR_ROWS * n_basis * PAD, 128), F32),
                pltpu.VMEM((POLAR_ROWS * n_basis * PAD, channels), F32),
                dma((peers - 1, CHUNKS)), dma((peers - 1, CHUNKS)),
                dma((PIECES - 1, peers - 1, CHUNKS)), dma((PIECES - 1, peers - 1, CHUNKS)),
                dma((peers, CHUNKS)), dma((peers, CHUNKS)),
                dma((2,)), dma((2,)), dma((2,)), dma((2,)),
                dma((peers - 1,)), dma((peers - 1,)), dma((peers,)), dma((peers,)), dma(()),
            ],
            compiler_params=pltpu.CompilerParams(
                collective_id=0, has_side_effects=True, vmem_limit_bytes=60 * 1024 * 1024
            ),
        )(signal, band_rows, support_rows, support_lons, table, mixing)

    placed = (P("lat", "lon", None), P(), P(), P(), P(), P(None, "lon", None))
    return jax.shard_map(
        per_device, mesh=mesh, in_specs=placed, out_specs=P("lat", "lon", None), check_vma=False
    )
```

```python
import functools

import jax
import jax.numpy as jnp
from jax import lax
from jax.experimental import pallas as pl
from jax.experimental.pallas import tpu as pltpu
from jax.sharding import PartitionSpec as P

LAT_REACH = 2
LON_REACH = 2
POLAR_ROWS = 2
SPAN = POLAR_ROWS + LAT_REACH
GROUP = 4
PAD = 24
WIDE = 32
PIECES = 4
CHUNKS = 3
POLAR_PAD = 80
MESH = pl.DeviceIdType.MESH
BF16 = jnp.bfloat16
F32 = jnp.float32


def rdma(src, dst, send_sem, recv_sem, lat, lon):
    return pltpu.make_async_remote_copy(
        src_ref=src, dst_ref=dst, send_sem=send_sem, recv_sem=recv_sem,
        device_id=(lat, lon), device_id_type=MESH,
    )


def kernel(
    n_lat, n_lon, grid_rows,
    signal, band_rows, sup_rows, sup_lons, basis, mixing, out,
    full_w, a_band, z_all, acc, ext, rim_send, rim_up, rim_down,
    edge_send, edge_recv, pol_send, pol, a_pol, z_pol,
    s1_send, s1_recv, s2_send, s2_recv, s3_send, s3_recv,
    rim_ss, rim_rs, edge_ss, edge_rs, p1_ss, p1_rs, p2_ss, p2_rs, own_sem,
):
    rows_dev, lon_dev, channels = signal.shape
    n_basis, c_dev, _ = mixing.shape
    support = sup_rows.shape[0]
    cycle = lon_dev * n_lon
    n_group = rows_dev // GROUP
    lat = lax.axis_index("lat")
    lon = lax.axis_index("lon")
    is_top = lat == 0
    is_bottom = lat == n_lat - 1
    is_polar = is_top | is_bottom
    sub = lat % PIECES
    lat_base = lat - sub
    peers = n_lon // 2
    partner = lon + 1 - 2 * (lon % 2)
    right = (lon + 1) % n_lon
    left = (lon + n_lon - 1) % n_lon
    ks = n_basis // CHUNKS

    live = band_rows[lat]
    first_row = 0
    for b in range(n_lat):
        first_row = first_row + jnp.where(b < lat, band_rows[b], 0)

    barrier = pltpu.get_barrier_semaphore()
    for d in range(1, peers):
        pl.semaphore_signal(barrier, inc=1, device_id=(lat, (lon + 2 * d) % n_lon), device_id_type=MESH)
    for e in range(1, PIECES):
        pl.semaphore_signal(barrier, inc=1, device_id=(lat_base + (sub + e) % PIECES, lon), device_id_type=MESH)
    pl.semaphore_signal(barrier, inc=1, device_id=(lat, right), device_id_type=MESH)
    pl.semaphore_signal(barrier, inc=1, device_id=(lat, left), device_id_type=MESH)

    @pl.when(lat > 0)
    def _():
        pl.semaphore_signal(barrier, inc=1, device_id=(lat - 1, lon), device_id_type=MESH)

    @pl.when(lat < n_lat - 1)
    def _():
        pl.semaphore_signal(barrier, inc=1, device_id=(lat + 1, lon), device_id_type=MESH)

    rim_send[...] = signal[pl.ds(jnp.clip(live - LAT_REACH, 0, rows_dev - LAT_REACH), LAT_REACH)]
    polar_start = jnp.where(is_bottom, jnp.clip(live - SPAN, 0, rows_dev - SPAN), 0)
    pol_rows = [signal[polar_start + r] for r in range(SPAN)]
    tail = jnp.zeros((POLAR_PAD - SPAN * lon_dev, channels), BF16)
    pol_send[...] = jnp.concatenate(pol_rows + [tail], axis=0)
    for r in range(rows_dev):
        edge_send[0, r] = signal[r, 0:LON_REACH]
        edge_send[1, r] = signal[r, lon_dev - LON_REACH : lon_dev]

    greeted = (peers - 1) + (PIECES - 1) + 2
    pl.semaphore_wait(barrier, greeted + jnp.where(lat > 0, 1, 0) + jnp.where(lat < n_lat - 1, 1, 0))

    def rows_of(source):
        return pl.ds(pl.multiple_of(source * c_dev, c_dev), c_dev)

    def lanes_of(piece):
        return pl.ds(pl.multiple_of(piece * 128, 128), 128)

    mine = rows_of(lon)
    q = lanes_of(sub)

    def stage1(d, j):
        kk = pl.ds(j * ks, ks)
        return rdma(
            mixing.at[kk, :, q], full_w.at[kk, mine, q], s1_send.at[d - 1, j], s1_recv.at[d - 1, j],
            lat, (lon + 2 * d) % n_lon,
        )

    def stage2(e, d, j):
        kk = pl.ds(j * ks, ks)
        region = full_w.at[kk, rows_of((lon + n_lon - 2 * d) % n_lon), q]
        return rdma(
            region, region, s2_send.at[e - 1, d - 1, j], s2_recv.at[e - 1, d - 1, j],
            lat_base + (sub + e) % PIECES, lon,
        )

    def stage3(d, j):
        kk = pl.ds(j * ks, ks)
        region = full_w.at[kk, rows_of((lon + n_lon - 2 * d) % n_lon), :]
        source = mixing.at[kk] if d == 0 else region
        return rdma(source, region, s3_send.at[d, j], s3_recv.at[d, j], lat, partner)

    up_copy = rdma(signal.at[pl.ds(0, LAT_REACH)], rim_down, rim_ss.at[0], rim_rs.at[0], lat - 1, lon)
    down_copy = rdma(rim_send, rim_up, rim_ss.at[1], rim_rs.at[1], lat + 1, lon)

    @pl.when(lat > 0)
    def _():
        up_copy.start()

    @pl.when(lat < n_lat - 1)
    def _():
        down_copy.start()

    for j in range(CHUNKS):
        for d in range(1, peers):
            stage1(d, j).start()
        stage3(0, j).start()
    own_copy = pltpu.make_async_copy(mixing, full_w.at[:, mine, :], own_sem)
    own_copy.start()

    def polar1(d):
        return rdma(pol_send, pol.at[lon, pl.ds(0, POLAR_PAD)], p1_ss.at[d - 1], p1_rs.at[d - 1], lat, (lon + 2 * d) % n_lon)

    def polar2(d):
        region = pol.at[(lon + n_lon - 2 * d) % n_lon, pl.ds(0, POLAR_PAD)]
        source = pol_send if d == 0 else region
        return rdma(source, region, p2_ss.at[d], p2_rs.at[d], lat, partner)

    @pl.when(is_top)
    def _():
        rim_up[...] = jnp.zeros_like(rim_up)

    @pl.when(is_bottom)
    def _():
        rim_down[...] = jnp.zeros_like(rim_down)

    @pl.when(is_polar)
    def _():
        for d in range(1, peers):
            polar1(d).start()
        polar2(0).start()
        pol[lon, pl.ds(0, POLAR_PAD)] = pol_send[...]
        for b in range(n_lon):
            pol[b, pl.ds(POLAR_PAD, 128 - POLAR_PAD)] = jnp.zeros((128 - POLAR_PAD, channels), BF16)

    col = lax.broadcasted_iota(jnp.int32, (PAD, 128), 1)
    pos = lax.broadcasted_iota(jnp.int32, (PAD, 128), 0)
    within = col % WIDE
    target = jnp.where(within < lon_dev, within, jnp.where(within < lon_dev + LON_REACH, within - lon_dev - LON_REACH, within - LON_REACH))
    code0 = jnp.where(within < lon_dev + 2 * LON_REACH, (col // WIDE) * 64 + target - pos + LON_REACH, -100000)
    half_rows = 128 // WIDE

    def accumulate(code, keys, grid_id):
        sums = [jnp.zeros((PAD, 128), F32) for _ in range(n_basis)]
        for s in range(support):
            hit = code == keys[s]
            for k in range(n_basis):
                sums[k] = sums[k] + jnp.where(hit, basis[k * support + s, grid_id], 0.0)
        return sums

    def build_slot(i, carry):
        g = i // GROUP
        r = i % GROUP
        grid_id = jnp.minimum(first_row + i, grid_rows - 1)
        keys = []
        for s in range(support):
            off = sup_lons[s, grid_id]
            off = jnp.where(off > cycle // 2, off - cycle, off)
            window = sup_rows[s, grid_id] - first_row + LAT_REACH - g * GROUP
            keys.append(window * 64 + off + LON_REACH)
        for h in range(2):
            sums = accumulate(code0, [key - h * half_rows * 64 for key in keys], grid_id)
            for k in range(n_basis):
                a_band[g, k, pl.ds(pl.multiple_of(r * PAD, PAD), PAD), h * 128 : (h + 1) * 128] = sums[k]
        return carry

    def forward2(j):
        for d in range(1, peers):
            stage1(d, j).wait_recv()
            for e in range(1, PIECES):
                stage2(e, d, j).start()

    def forward3(j):
        for d in range(1, peers):
            for e in range(1, PIECES):
                stage2(e, d, j).wait_recv()
            stage3(d, j).start()

    lax.fori_loop(0, 4, build_slot, 0)

    @pl.when(lat > 0)
    def _():
        down_copy.wait_recv()

    @pl.when(lat < n_lat - 1)
    def _():
        up_copy.wait_recv()

    for r in range(LAT_REACH):
        edge_send[0, rows_dev + r] = rim_up[r, 0:LON_REACH]
        edge_send[1, rows_dev + r] = rim_up[r, lon_dev - LON_REACH : lon_dev]
        edge_send[0, rows_dev + LAT_REACH + r] = rim_down[r, 0:LON_REACH]
        edge_send[1, rows_dev + LAT_REACH + r] = rim_down[r, lon_dev - LON_REACH : lon_dev]
    lax.fori_loop(4, 6, build_slot, 0)
    to_left = rdma(edge_send.at[0], edge_recv.at[1], edge_ss.at[0], edge_rs.at[0], lat, left)
    to_right = rdma(edge_send.at[1], edge_recv.at[0], edge_ss.at[1], edge_rs.at[1], lat, right)
    to_left.start()
    to_right.start()
    forward2(0)
    lax.fori_loop(6, 14, build_slot, 0)
    forward2(1)
    lax.fori_loop(14, rows_dev, build_slot, 0)

    @pl.when(is_polar)
    def _():
        for d in range(1, peers):
            polar1(d).wait_recv()
            polar2(d).start()

    forward2(2)
    forward3(0)

    to_left.wait_recv()
    to_right.wait_recv()

    def source_row(slot, own, rim_u, rim_d):
        if slot < 0:
            return rim_u(slot + LAT_REACH)
        base = own(min(slot, rows_dev - 1))
        if slot < rows_dev // 2:
            return base
        value = jnp.where(live == slot, rim_d(0), base)
        return jnp.where(live + 1 == slot, rim_d(1), value)

    filler = jnp.zeros((WIDE - lon_dev - 2 * LON_REACH, channels), BF16)
    for e in range(rows_dev + 2 * LAT_REACH):
        centre = source_row(e - LAT_REACH, lambda r: signal[r], lambda r: rim_up[r], lambda r: rim_down[r])
        sides = [
            source_row(
                e - LAT_REACH,
                lambda r: edge_recv[side, r],
                lambda r: edge_recv[side, rows_dev + r],
                lambda r: edge_recv[side, rows_dev + LAT_REACH + r],
            )
            for side in range(2)
        ]
        ext[e] = jnp.concatenate([centre, sides[0], sides[1], filler], axis=0)

    out_base = jnp.where(is_bottom, grid_rows - POLAR_ROWS, 0)
    src_base = jnp.where(is_bottom, grid_rows - SPAN, 0)

    @pl.when(is_polar)
    def _():
        for d in range(peers):
            polar2(d).wait_recv()
        z_pol[...] = jnp.zeros_like(z_pol)
        prow = jnp.where(col >= lon_dev, 1, 0) + jnp.where(col >= 2 * lon_dev, 1, 0) + jnp.where(col >= 3 * lon_dev, 1, 0)
        pcol = col - prow * lon_dev

        def polar_block(b, carry):
            shift = pcol - pos + (b - lon) * lon_dev
            shift = jnp.where(shift < 0, shift + cycle, shift)
            code = jnp.where(col < SPAN * lon_dev, prow * cycle + shift, -100000)
            for r in range(POLAR_ROWS):
                grid_id = out_base + r
                keys = [(sup_rows[s, grid_id] - src_base) * cycle + sup_lons[s, grid_id] for s in range(support)]
                sums = accumulate(code, keys, grid_id)
                for k in range(n_basis):
                    a_pol[pl.ds((r * n_basis + k) * PAD, PAD), :] = sums[k]
            z_pol[...] += jnp.dot(a_pol[...].astype(BF16), pol[b], preferred_element_type=F32)
            return carry

        lax.fori_loop(0, n_lon, polar_block, 0)

    forward3(1)
    polar_slot = jnp.where(is_top, 0, jnp.where(is_bottom, live - POLAR_ROWS, -100))
    span_rows = GROUP * PAD
    group_slot = lax.broadcasted_iota(jnp.int32, (span_rows, channels), 0) // PAD

    def apply_group(g, carry):
        a_now = a_band[g].reshape(n_basis * span_rows, 256).astype(BF16)
        window = ext[pl.ds(g * GROUP, 2 * GROUP)].reshape(256, channels)
        terms = jnp.dot(a_now, window, preferred_element_type=F32)
        for k in range(n_basis):
            value = terms[k * span_rows : (k + 1) * span_rows]
            for r in range(POLAR_ROWS):
                chosen = z_pol[pl.ds((r * n_basis + k) * PAD, PAD), :]
                chosen = jnp.concatenate([chosen] * GROUP, axis=0)
                value = jnp.where(group_slot == polar_slot + r - g * GROUP, chosen, value)
            z_all[pl.ds(pl.multiple_of(g * span_rows, span_rows), span_rows), k * channels : (k + 1) * channels] = value.astype(BF16)
        return carry

    lax.fori_loop(0, n_group, apply_group, 0)
    forward3(2)

    own_copy.wait()
    half_m = rows_dev * PAD // 2
    acc[...] = jnp.zeros_like(acc)
    for j in range(CHUNKS):
        for d in range(peers):
            stage3(d, j).wait_recv()

        def mix(t, carry):
            k = j * ks + t // 2
            rows = pl.ds(pl.multiple_of((t % 2) * half_m, half_m), half_m)
            lhs = z_all[rows, pl.ds(pl.multiple_of(k * channels, channels), channels)]
            acc[rows, :] += jnp.dot(lhs, full_w[k], preferred_element_type=F32)
            return carry

        lax.fori_loop(0, 2 * ks, mix, 0)

    def put(i, carry):
        value = acc[pl.ds(pl.multiple_of(i * PAD, PAD), PAD), :]
        value = jnp.where(i < live, value, 0.0)
        out[i] = value[0:lon_dev].astype(BF16)
        return carry

    lax.fori_loop(0, rows_dev, put, 0)

    to_left.wait_send()
    to_right.wait_send()

    @pl.when(lat > 0)
    def _():
        up_copy.wait_send()

    @pl.when(lat < n_lat - 1)
    def _():
        down_copy.wait_send()

    @pl.when(is_polar)
    def _():
        for d in range(peers):
            if d:
                polar1(d).wait_send()
            polar2(d).wait_send()

    for j in range(CHUNKS):
        for d in range(peers):
            stage3(d, j).wait_send()
            if d:
                stage1(d, j).wait_send()
                for e in range(1, PIECES):
                    stage2(e, d, j).wait_send()


def solution(mesh):
    n_lat, n_lon = mesh.shape["lat"], mesh.shape["lon"]

    def per_device(signal, band_rows, support_rows, support_lons, basis_values, mixing):
        rows_dev, lon_dev, channels = signal.shape
        n_basis, c_dev, outs = mixing.shape
        grid_rows, support = support_rows.shape
        peers = n_lon // 2
        table = jnp.transpose(basis_values, (2, 1, 0)).astype(F32).reshape(n_basis * support, grid_rows)
        vmem = pl.BlockSpec(memory_space=pltpu.VMEM)
        smem = pl.BlockSpec(memory_space=pltpu.SMEM)
        dma = pltpu.SemaphoreType.DMA
        return pl.pallas_call(
            functools.partial(kernel, n_lat, n_lon, grid_rows),
            out_shape=jax.ShapeDtypeStruct((rows_dev, lon_dev, outs), BF16),
            in_specs=[vmem, smem, smem, smem, smem, vmem],
            out_specs=vmem,
            scratch_shapes=[
                pltpu.VMEM((n_basis, n_lon * c_dev, outs), BF16),
                pltpu.VMEM((rows_dev // GROUP, n_basis, GROUP * PAD, 256), F32),
                pltpu.VMEM((rows_dev * PAD, n_basis * channels), BF16),
                pltpu.VMEM((rows_dev * PAD, outs), F32),
                pltpu.VMEM((rows_dev + 2 * LAT_REACH, WIDE, channels), BF16),
                pltpu.VMEM((LAT_REACH, lon_dev, channels), BF16),
                pltpu.VMEM((LAT_REACH, lon_dev, channels), BF16),
                pltpu.VMEM((LAT_REACH, lon_dev, channels), BF16),
                pltpu.VMEM((2, rows_dev + 2 * LAT_REACH, LON_REACH, channels), BF16),
                pltpu.VMEM((2, rows_dev + 2 * LAT_REACH, LON_REACH, channels), BF16),
                pltpu.VMEM((POLAR_PAD, channels), BF16),
                pltpu.VMEM((n_lon, 128, channels), BF16),
                pltpu.VMEM((POLAR_ROWS * n_basis * PAD, 128), F32),
                pltpu.VMEM((POLAR_ROWS * n_basis * PAD, channels), F32),
                dma((peers - 1, CHUNKS)), dma((peers - 1, CHUNKS)),
                dma((PIECES - 1, peers - 1, CHUNKS)), dma((PIECES - 1, peers - 1, CHUNKS)),
                dma((peers, CHUNKS)), dma((peers, CHUNKS)),
                dma((2,)), dma((2,)), dma((2,)), dma((2,)),
                dma((peers - 1,)), dma((peers - 1,)), dma((peers,)), dma((peers,)), dma(()),
            ],
            compiler_params=pltpu.CompilerParams(
                collective_id=0, has_side_effects=True, vmem_limit_bytes=60 * 1024 * 1024
            ),
        )(signal, band_rows, support_rows.T, support_lons.T, table, mixing)

    placed = (P("lat", "lon", None), P(), P(), P(), P(), P(None, "lon", None))
    return jax.shard_map(
        per_device, mesh=mesh, in_specs=placed, out_specs=P("lat", "lon", None), check_vma=False
    )
```
